32 devices in a mesh: band: 4 (over x, core), slab: 8 (over z, y).
Axes of the slice: x: 2, y: 2, z: 4, core: 2. Of those that a mesh axis runs over, the one named last changes fastest.
Arguments:
- orbitals: float32 [16, 128, 128, 128], P('band', 'slab'), may hold values from -6 to 6
- occupations: float32 [16], P('band'), may hold values from 0.1 to 1
- accumulated: float32 [16, 128, 128, 128], P('band', 'slab'), may hold values from -6 to 6
Outputs:
- exchange_terms: float32 [16, 128, 128, 128], P('band', 'slab')
The draws below stay inside these ranges and needn't reach their ends.
All inputs are finite; a program needn't handle non-finite values.
Results may differ from the reference program's by a relative error of at most 0.00012.
Values sent between devices are 32-bit elements; how exact they have to be, the bound alone decides.
No kernel may reach another device: no remote copies, remote signals or barrier semaphores. Data moves between devices by JAX's collectives and lax.ppermute only.
A program may use at most 128 MiB of HBM per device.

```python
import math
import jax
import jax.numpy as jnp
from jax import lax

GRID = 128
ORB_DEV = 4
HOPS = 3
ORBITALS = 16
N_BAND = 4


def shard_levels(own_key, shape, shards, smallest, top_value):
    loudness, own = 1.0, jax.random.fold_in(own_key, 6)
    for dim, shards_of in shards:
        draws = jnp.exp(jax.random.uniform(jax.random.fold_in(own, dim), (shards_of,), jnp.float32, smallest / len(shards), top_value / len(shards)))
        loudness = loudness * jnp.repeat(draws, shape[dim] // shards_of).reshape([-1 if axis == dim else 1 for axis in range(len(shape))])
    return loudness


def bell_draw(rng, extent, width, reach, shards=(), kind=jnp.bfloat16):
    drawn = jax.random.normal(rng, extent, jnp.float32) * width
    if len(shards) > 0:
        drawn = shard_levels(rng, extent, shards, -0.22, 0.18) * drawn
    return jnp.clip(drawn, min=-reach, max=reach).astype(kind)


def setup_inputs(seed: int = 0) -> dict:
    seeds = jax.random.split(jax.random.key(seed), 4)
    return {
        "orbitals": bell_draw(seeds[0], (ORBITALS, GRID, GRID, GRID), 1.0, 6.0, ((0, 4), (1, 8)), jnp.float32),
        "occupations": jnp.clip(jnp.exp(math.log(1.0) - 2.3025851 * jax.random.uniform(seeds[1], (ORBITALS,), jnp.float32) ** shard_levels(seeds[1], (ORBITALS,), ((0, 4),), -0.2, 0.2)), 0.1, 1.0),
        "accumulated": bell_draw(seeds[2], (ORBITALS, GRID, GRID, GRID), 1.0, 6.0, ((0, 4), (1, 8)), jnp.float32),
    }


def kernel_grid():
    index = jnp.arange(GRID, dtype=jnp.int32)
    signed = jnp.where(index < GRID // 2, index, index - GRID)
    wave = signed.astype(jnp.float32) * (2.0 * math.pi / GRID)
    square = wave[:, None, None] ** 2 + wave[None, :, None] ** 2 + wave[None, None, :] ** 2
    return 4.0 * math.pi / (square + 0.01)


def reference(orbitals, occupations, accumulated):
    screening = kernel_grid()
    visitors = orbitals[::ORB_DEV]
    visitor_occ = occupations[::ORB_DEV]
    owner = jnp.arange(ORBITALS, dtype=jnp.int32) // ORB_DEV
    result = accumulated
    for travel in range(1, HOPS + 1):
        source = ((owner - travel) % N_BAND).astype(jnp.int32)

        def pair_term(items):
            resident, which = items
            visitor = visitors[which]
            spectrum = jnp.fft.fftn(resident * visitor)
            potential = jnp.real(jnp.fft.ifftn(screening * spectrum)).astype(resident.dtype)
            return visitor_occ[which] * visitor * potential

        result = result - lax.map(pair_term, (orbitals, source))
    return result
```

```python
import functools
import math

import jax
import jax.numpy as jnp
from jax import lax
from jax.experimental import pallas as pl
from jax.experimental.pallas import tpu as pltpu
from jax.sharding import PartitionSpec as P

HOPS = 3
CORES = 2
AXES = ("band", "slab")


def shifted(value, axis, steps):
    count = lax.axis_size(axis)
    pairs = [(source, (source + steps) % count) for source in range(count)]
    return lax.ppermute(value, axis, pairs)


def hartley_rows(rows, extent):
    index = jnp.arange(extent, dtype=jnp.int32)
    product = rows[:, None] * index[None, :] % extent
    angle = product.astype(jnp.float32) * (2.0 * math.pi / extent)
    return jnp.cos(angle) + jnp.sin(angle)


def hartley_matrix(extent):
    return hartley_rows(jnp.arange(extent, dtype=jnp.int32), extent)


def signed_wave(index, extent):
    signed = jnp.where(index < extent // 2, index, index - extent)
    return signed.astype(jnp.float32) * (2.0 * math.pi / extent)


def slab_body(orbitals, occupations, accumulated):
    extent = orbitals.shape[2]
    planes = orbitals.shape[1]
    matrix = hartley_matrix(extent)
    full_index = jnp.arange(extent, dtype=jnp.int32)
    local_index = lax.axis_index("slab") * planes + jnp.arange(planes, dtype=jnp.int32)
    wave_full = signed_wave(full_index, extent)
    wave_local = signed_wave(local_index, extent)
    square = (
        wave_full[:, None, None] ** 2
        + wave_local[None, :, None] ** 2
        + wave_full[None, None, :] ** 2
    )
    screening = 4.0 * math.pi / (square + 0.01) / float(extent**3)
    highest = lax.Precision.HIGHEST

    def transform_inner(values):
        spectra = jnp.einsum("pxyz,zc->pxyc", values, matrix, precision=highest)
        return jnp.einsum("pxyc,yb->pxbc", spectra, matrix, precision=highest)

    leading = orbitals[0]
    leading_occ = occupations[0:1]
    carried = (leading, leading_occ)
    visits = []
    for travel in range(HOPS):
        carried = shifted((carried[0], carried[1]), "band", 1)
        visits.append(carried)
    result = accumulated
    for visitor, visitor_occ in visits:
        potentials_spectra = transform_inner(orbitals * visitor[None])
        columns = jnp.einsum(
            "pxbc,xa->pabc",
            lax.all_to_all(potentials_spectra, "slab", split_axis=2, concat_axis=1, tiled=True),
            matrix,
            precision=highest,
        )
        columns = columns * screening[None]
        columns = jnp.einsum("pabc,ax->pxbc", columns, matrix, precision=highest)
        returned = lax.all_to_all(columns, "slab", split_axis=1, concat_axis=2, tiled=True)
        potential = transform_inner(returned)
        result = result - visitor_occ[0] * visitor[None] * potential
    return result


def halves(values):
    head = values.astype(jnp.bfloat16)
    return head, (values - head.astype(jnp.float32)).astype(jnp.bfloat16)


def rounded_halves(matrix):
    head = lax.reduce_precision(matrix, exponent_bits=8, mantissa_bits=7)
    return head.astype(jnp.bfloat16), (matrix - head).astype(jnp.bfloat16)


def right_factor(matrix):
    head, tail = rounded_halves(matrix)
    return jnp.concatenate(
        [
            jnp.concatenate([head, tail], 1),
            jnp.concatenate([head, jnp.zeros_like(tail)], 1),
        ],
        0,
    )


def left_factor(matrix):
    head, tail = rounded_halves(matrix)
    return jnp.concatenate(
        [
            jnp.concatenate([head, head], 1),
            jnp.concatenate([tail, jnp.zeros_like(tail)], 1),
        ],
        0,
    )


def times_right(rows, factor):
    width = rows.shape[1]
    out = jnp.dot(
        jnp.concatenate(halves(rows), 1), factor, preferred_element_type=jnp.float32
    )
    return out[:, :width] + out[:, width:]


def times_left(factor, columns):
    out = jnp.dot(
        factor, jnp.concatenate(halves(columns), 0), preferred_element_type=jnp.float32
    )
    height = out.shape[0] // 2
    return out[:height] + out[height:]


def forward_kernel(flag_ref, *refs):
    slots = 4
    near = refs[:slots]
    residents = refs[slots : 2 * slots]
    right_ref, left_ref, kept_ref, sent_ref = refs[2 * slots :]
    keep = kept_ref.shape[0]
    depth, extent, width = near[0].shape
    flip = flag_ref[0] == 1
    for slot in range(slots):
        base = slot - slot % 2
        own, other = residents[base + slot % 2], residents[base + 1 - slot % 2]
        made = []
        for plane in range(0, depth, 2):
            pair = []
            for p in (plane, plane + 1):
                resident = jnp.where(flip, other[p], own[p])
                pair.append(times_right(resident * near[slot][p], right_ref[...]))
            both = times_left(left_ref[...], jnp.concatenate(pair, 1))
            made.append(both[:, :width])
            made.append(both[:, width:])
        block = jnp.stack(made, 0)
        swapped = jnp.transpose(block, (1, 0, 2))
        kept_ref[:, slot * depth : (slot + 1) * depth, :] = swapped[:keep]
        sent_ref[:, slot * depth : (slot + 1) * depth, :] = swapped[keep:]


def across_kernel(a_ref, b_ref, c_ref, d_ref, screen_ref, forth_ref, back_ref, *outs):
    parts = (a_ref, b_ref, c_ref, d_ref)
    count, depth, width = a_ref.shape
    for row in range(0, count, 2):
        columns = jnp.concatenate(
            [
                jnp.concatenate([part[row], part[row + 1]], 1)
                for part in parts
            ],
            0,
        )
        spectrum = times_left(forth_ref[...], columns)
        spectrum = spectrum * jnp.concatenate([screen_ref[row], screen_ref[row + 1]], 1)
        lines = times_left(back_ref[...], spectrum)
        for index, out in enumerate(outs):
            out[row] = lines[index * depth : (index + 1) * depth, :width]
            out[row + 1] = lines[index * depth : (index + 1) * depth, width:]


def inverse_kernel(first, flag_ref, weight_ref, own_ref, other_ref, *refs):
    slots = 4
    near = refs[:slots]
    refs = refs[slots:]
    sums = () if first else refs[:slots]
    right_ref, left_ref = refs[len(sums) : len(sums) + 2]
    outs = refs[len(sums) + 2 :]
    depth, extent, width = near[0].shape
    flip = flag_ref[0] == 1
    weight = weight_ref[0]
    for slot in range(slots):
        rows = jnp.concatenate(
            [
                own_ref[:, slot * depth : (slot + 1) * depth, :],
                other_ref[:, slot * depth : (slot + 1) * depth, :],
            ],
            0,
        )
        rows = times_right(rows.reshape(extent * depth, width), right_ref[...])
        block = jnp.transpose(rows.reshape(extent, depth, width), (1, 0, 2))
        base = slot - slot % 2
        for plane in range(0, depth, 2):
            both = times_left(
                left_ref[...], jnp.concatenate([block[plane], block[plane + 1]], 1)
            )
            for offset in range(2):
                p = plane + offset
                potential = both[:, offset * width : (offset + 1) * width]
                term = weight * near[slot][p] * potential

                def put(to):
                    outs[to][p] = term if first else term + sums[to][p]

                @pl.when(jnp.logical_not(flip))
                def _():
                    put(base + slot % 2)

                @pl.when(flip)
                def _():
                    put(base + 1 - slot % 2)


def vmem(count):
    return [pl.BlockSpec(memory_space=pltpu.VMEM)] * count


def smem(count):
    return [pl.BlockSpec(memory_space=pltpu.SMEM)] * count


def chip_body(orbitals, occupations, accumulated):
    residents, planes, extent, width = orbitals.shape
    bands, slabs = lax.axis_size("band"), lax.axis_size("slab")
    lines = slabs // 2
    depth = planes // CORES
    band, slab = lax.axis_index("band"), lax.axis_index("slab")
    core, side = band % CORES, slab % 2
    line = slab // 2

    def moved(value, to):
        pairs = []
        for x in range(bands // CORES):
            for c in range(CORES):
                for z in range(lines):
                    for y in range(2):
                        target = to(x, c, z, y)
                        if target is not None:
                            tx, tc, tz, ty = target
                            pairs.append(
                                (
                                    (x * CORES + c) * slabs + z * 2 + y,
                                    (tx * CORES + tc) * slabs + tz * 2 + ty,
                                )
                            )
        return lax.ppermute(value, AXES, pairs)

    over_core = lambda x, c, z, y: (x, c ^ 1, z, y)
    over_x = lambda x, c, z, y: (x ^ 1, c, z, y)
    over_y = lambda x, c, z, y: (x, c, z, y ^ 1)
    over_z = lambda x, c, z, y: (x, c, z ^ 1, y)
    over_middle = lambda x, c, z, y: (x, c, z ^ 3, y) if z in (1, 2) else None
    outward = lambda x, c, z, y: (x, c, z ^ 1, y) if z in (1, 2) else None

    def piece(orbital, half):
        return lax.dynamic_slice(
            orbitals, (orbital, half * depth, 0, 0), (1, depth, extent, width)
        )[0]

    zero = jnp.int32(0)
    kept_half = piece(zero, core)
    swapped_half = moved(piece(zero, 1 - core), over_core)
    same = core == side
    mine = [jnp.where(same, kept_half, swapped_half)]
    next_ = [jnp.where(same, swapped_half, kept_half)]

    def shares(bits):
        return moved(occupations[0:1], lambda x, c, z, y: (x ^ (bits // 2), c ^ (bits % 2), z, y))

    all_shares = jnp.concatenate([occupations[0:1]] + [shares(bits) for bits in range(1, bands)])

    def share(x_bit, owner):
        return lax.dynamic_slice(all_shares, (x_bit * 2 + (core ^ owner),), (1,))

    held = [[None, None] for _ in range(lines)]

    def fetch(m):
        for t in range(2):
            held[m][t] = moved(
                piece(line ^ m, core ^ side ^ t),
                lambda x, c, z, y, m=m, t=t: (x, c ^ y ^ t, z ^ m, c),
            )

    mine.append(moved(mine[0], over_z))
    next_.append(moved(next_[0], over_z))
    fetch(0)
    fetch(1)
    fetch(2)
    fetch(3)
    middle = (line == 1) | (line == 2)
    for group in (mine, next_):
        inner = [moved(group[m], over_middle) for m in range(2)]
        outer = [moved(value, outward) for value in inner]
        group.append(jnp.where(middle, inner[1], outer[0]))
        group.append(jnp.where(middle, inner[0], outer[1]))
    far_mine = [moved(value, over_x) for value in mine]
    far_next = [moved(value, over_x) for value in next_]
    next_beside = [moved(value, over_y) for value in mine]
    far_next_beside = [moved(value, over_x) for value in next_beside]
    far_mine_beside = [moved(value, over_y) for value in far_next]
    visitors = [
        (next_, next_beside, share(0, 1 - side)),
        (far_mine, far_mine_beside, share(1, side)),
        (far_next, far_next_beside, share(1, 1 - side)),
    ]

    natural = jnp.arange(extent, dtype=jnp.int32)
    matrix = hartley_matrix(extent)
    keep = extent // CORES
    order_b = (natural + core * keep) % extent
    steps = jnp.arange(lines, dtype=jnp.int32)
    sides = jnp.arange(2, dtype=jnp.int32)
    offsets = jnp.arange(depth, dtype=jnp.int32)
    spots = (
        (line ^ steps)[:, None, None] * (2 * planes)
        + (side ^ sides)[None, :, None] * planes
        + offsets[None, None, :]
    ).reshape(-1)
    order_x = jnp.concatenate([spots + core * depth, spots + (1 - core) * depth])
    rows_b = hartley_rows(order_b, extent)
    rows_x = hartley_rows(order_x, extent)
    right = right_factor(matrix)
    left_b_forth = left_factor(rows_b)
    left_b_back = left_factor(rows_b.T)
    left_x_forth = left_factor(rows_x.T)
    left_x_back = left_factor(rows_x)
    wave = signed_wave(natural, extent)
    wave_b = signed_wave(order_b[:keep], extent)
    square = wave_b[:, None, None] ** 2 + wave[None, :, None] ** 2 + wave[None, None, :] ** 2
    screen = 4.0 * math.pi / (square + 0.01) / float(extent**3)

    flag = core.reshape(1).astype(jnp.int32)
    group = lines // 2 * 2 * depth
    spectrum_shape = jax.ShapeDtypeStruct((keep, group, width), jnp.float32)
    piece_shape = jax.ShapeDtypeStruct((depth, extent, width), jnp.float32)
    ranges = ((0, 1), (2, 3))

    def gather_four(table, beside, ms):
        return [value for m in ms for value in (table[m], beside[m])]

    def held_four(table, ms):
        return [value for m in ms for value in table[m]]

    params = pltpu.CompilerParams(vmem_limit_bytes=48 * 1024 * 1024)

    def forward(visitor, ms):
        near, beside, _ = visitor
        return pl.pallas_call(
            forward_kernel,
            out_shape=(spectrum_shape, spectrum_shape),
            in_specs=smem(1) + vmem(10),
            out_specs=tuple(vmem(2)),
            compiler_params=params,
            name="forward",
        )(flag, *gather_four(near, beside, ms), *held_four(held, ms), right, left_b_forth)

    def across(parts):
        return pl.pallas_call(
            across_kernel,
            out_shape=(spectrum_shape,) * 4,
            in_specs=vmem(7),
            out_specs=tuple(vmem(4)),
            compiler_params=params,
            name="across",
        )(*parts, screen, left_x_forth, left_x_back)

    def inverse(visitor, ms, own, other, sums):
        near, beside, weight = visitor
        extra = [] if sums is None else sums
        return pl.pallas_call(
            functools.partial(inverse_kernel, sums is None),
            out_shape=(piece_shape,) * 4,
            in_specs=smem(2) + vmem(2 + 4 + len(extra) + 2),
            out_specs=tuple(vmem(4)),
            compiler_params=params,
            name="inverse",
        )(flag, weight, own, other, *gather_four(near, beside, ms), *extra, right, left_b_back)

    totals = [None, None]
    for visitor in visitors:
        kept, got = [], []
        for ms in ranges:
            own, sent = forward(visitor, ms)
            kept.append(own)
            got.append(moved(sent, over_core))
        lines_out = across(kept + got)
        for index, ms in enumerate(ranges):
            back = moved(lines_out[2 + index], over_core)
            totals[index] = list(inverse(visitor, ms, lines_out[index], back, totals[index]))

    result = accumulated
    for index, ms in reversed(list(enumerate(ranges))):
        for place, m in enumerate(ms):
            for t in range(2):
                back = moved(
                    totals[index][2 * place + t],
                    lambda x, c, z, y, m=m, t=t: (x, y, z ^ m, c ^ y ^ t),
                )
                start = (line ^ m, (core ^ side ^ t) * depth, 0, 0)
                old = lax.dynamic_slice(accumulated, start, (1, depth, extent, width))
                result = lax.dynamic_update_slice(result, old - back[None], start)
    return result


def solution(mesh):
    bands, slabs = mesh.shape["band"], mesh.shape["slab"]

    def body(orbitals, occupations, accumulated):
        residents, planes = orbitals.shape[:2]
        one_each = bands == HOPS + 1 and slabs == 2 * residents and residents == 2 * CORES
        if one_each and planes % (8 * CORES) == 0:
            return chip_body(orbitals, occupations, accumulated)
        return slab_body(orbitals, occupations, accumulated)

    in_specs = (P("band", "slab", None, None), P("band"), P("band", "slab", None, None))
    out_specs = P("band", "slab", None, None)
    return jax.shard_map(body, mesh=mesh, in_specs=in_specs, out_specs=out_specs, check_vma=False)
```

```python
import math

import jax
import jax.numpy as jnp
from jax import lax
from jax.experimental import pallas as pl
from jax.experimental.pallas import tpu as pltpu
from jax.sharding import PartitionSpec as P


HOPS = 3
CORES = 2
AXES = ("band", "slab")


def shifted(value, axis, steps):
    count = lax.axis_size(axis)
    pairs = [(source, (source + steps) % count) for source in range(count)]
    return lax.ppermute(value, axis, pairs)


def hartley_rows(rows, extent):
    index = jnp.arange(extent, dtype=jnp.int32)
    product = rows[:, None] * index[None, :] % extent
    angle = product.astype(jnp.float32) * (2.0 * math.pi / extent)
    return jnp.cos(angle) + jnp.sin(angle)


def hartley_matrix(extent):
    return hartley_rows(jnp.arange(extent, dtype=jnp.int32), extent)


def signed_wave(index, extent):
    signed = jnp.where(index < extent // 2, index, index - extent)
    return signed.astype(jnp.float32) * (2.0 * math.pi / extent)


def slab_body(orbitals, occupations, accumulated):
    extent = orbitals.shape[2]
    planes = orbitals.shape[1]
    matrix = hartley_matrix(extent)
    full_index = jnp.arange(extent, dtype=jnp.int32)
    local_index = lax.axis_index("slab") * planes + jnp.arange(planes, dtype=jnp.int32)
    wave_full = signed_wave(full_index, extent)
    wave_local = signed_wave(local_index, extent)
    square = (
        wave_full[:, None, None] ** 2
        + wave_local[None, :, None] ** 2
        + wave_full[None, None, :] ** 2
    )
    screening = 4.0 * math.pi / (square + 0.01) / float(extent**3)
    highest = lax.Precision.HIGHEST

    def transform_inner(values):
        spectra = jnp.einsum("pxyz,zc->pxyc", values, matrix, precision=highest)
        return jnp.einsum("pxyc,yb->pxbc", spectra, matrix, precision=highest)

    leading = orbitals[0]
    leading_occ = occupations[0:1]
    carried = (leading, leading_occ)
    visits = []
    for _ in range(HOPS):
        carried = shifted((carried[0], carried[1]), "band", 1)
        visits.append(carried)
    result = accumulated
    for visitor, visitor_occ in visits:
        potentials_spectra = transform_inner(orbitals * visitor[None])
        columns = jnp.einsum(
            "pxbc,xa->pabc",
            lax.all_to_all(potentials_spectra, "slab", split_axis=2, concat_axis=1, tiled=True),
            matrix,
            precision=highest,
        )
        columns = columns * screening[None]
        columns = jnp.einsum("pabc,ax->pxbc", columns, matrix, precision=highest)
        returned = lax.all_to_all(columns, "slab", split_axis=1, concat_axis=2, tiled=True)
        potential = transform_inner(returned)
        result = result - visitor_occ[0] * visitor[None] * potential
    return result


def halves(values):
    head = values.astype(jnp.bfloat16)
    return head, (values - head.astype(jnp.float32)).astype(jnp.bfloat16)


def rounded_halves(matrix):
    head = lax.reduce_precision(matrix, exponent_bits=8, mantissa_bits=7)
    return head.astype(jnp.bfloat16), (matrix - head).astype(jnp.bfloat16)


def right_factor(matrix):
    head, tail = rounded_halves(matrix)
    return jnp.concatenate(
        [
            jnp.concatenate([head, tail], 1),
            jnp.concatenate([head, jnp.zeros_like(tail)], 1),
        ],
        0,
    )


def left_factor(matrix):
    head, tail = rounded_halves(matrix)
    return jnp.concatenate(
        [
            jnp.concatenate([head, head], 1),
            jnp.concatenate([tail, jnp.zeros_like(tail)], 1),
        ],
        0,
    )


def times_right(rows, factor):
    width = rows.shape[1]
    out = jnp.dot(
        jnp.concatenate(halves(rows), 1), factor, preferred_element_type=jnp.float32
    )
    return out[:, :width] + out[:, width:]


def times_left(factor, columns):
    out = jnp.dot(
        factor, jnp.concatenate(halves(columns), 0), preferred_element_type=jnp.float32
    )
    height = out.shape[0] // 2
    return out[:height] + out[height:]


def forward_kernel(flag_ref, own_ref, beside_ref, *refs):
    residents = refs[:4]
    right_ref, left_ref, kept_ref, sent_ref = refs[4:]
    keep = kept_ref.shape[0]
    places, depth, _, width = own_ref.shape
    flip = flag_ref[0] == 1
    for place in range(places):
        first, second = residents[2 * place], residents[2 * place + 1]
        for e in range(2):
            visitor = (own_ref, beside_ref)[e]
            made = []
            for plane in range(0, depth, 2):
                pair = []
                for p in (plane, plane + 1):
                    if e == 0:
                        resident = jnp.where(flip, second[p], first[p])
                    else:
                        resident = jnp.where(flip, first[p], second[p])
                    pair.append(times_right(resident * visitor[place, p], right_ref[...]))
                both = times_left(left_ref[...], jnp.concatenate(pair, 1))
                made.append(both[:, :width])
                made.append(both[:, width:])
            block = jnp.transpose(jnp.stack(made, 0), (1, 0, 2))
            at = (2 * place + e) * depth
            kept_ref[:, at : at + depth, :] = block[:keep]
            sent_ref[:, at : at + depth, :] = block[keep:]


def across_kernel(a_ref, b_ref, c_ref, d_ref, screen_ref, forth_ref, back_ref, *outs):
    parts = (a_ref, b_ref, c_ref, d_ref)
    count, depth, width = a_ref.shape
    for row in range(0, count, 2):
        columns = jnp.concatenate(
            [
                jnp.concatenate([part[row], part[row + 1]], 1)
                for part in parts
            ],
            0,
        )
        spectrum = times_left(forth_ref[...], columns)
        spectrum = spectrum * jnp.concatenate([screen_ref[row], screen_ref[row + 1]], 1)
        lines = times_left(back_ref[...], spectrum)
        for index, out in enumerate(outs):
            out[row] = lines[index * depth : (index + 1) * depth, :width]
            out[row + 1] = lines[index * depth : (index + 1) * depth, width:]


def inverse_kernel(flag_ref, weight_ref, right_ref, left_ref, *refs):
    outs = refs[-4:]
    groups = [refs[4 * index : 4 * index + 4] for index in range(len(refs) // 4 - 1)]
    places, depth, extent, width = groups[0][2].shape
    flip = flag_ref[0] == 1

    def potentials(own_ref, other_ref, slot):
        at = slice(slot * depth, (slot + 1) * depth)
        rows = jnp.concatenate([own_ref[:, at, :], other_ref[:, at, :]], 0)
        rows = times_right(rows.reshape(extent * depth, width), right_ref[...])
        block = jnp.transpose(rows.reshape(extent, depth, width), (1, 0, 2))
        made = []
        for plane in range(0, depth, 2):
            both = times_left(
                left_ref[...], jnp.concatenate([block[plane], block[plane + 1]], 1)
            )
            made += [both[:, :width], both[:, width:]]
        return made

    for place in range(places):
        sums = [[None] * depth, [None] * depth]
        for e in range(2):
            for index, (own_ref, other_ref, near_ref, beside_ref) in enumerate(groups):
                made = potentials(own_ref, other_ref, 2 * place + e)
                visitor = (near_ref, beside_ref)[e]
                for p in range(depth):
                    term = weight_ref[index] * visitor[place, p] * made[p]
                    sums[e][p] = term if index == 0 else sums[e][p] + term
        for p in range(depth):
            outs[2 * place][p] = jnp.where(flip, sums[1][p], sums[0][p])
            outs[2 * place + 1][p] = jnp.where(flip, sums[0][p], sums[1][p])


def vmem(count):
    return [pl.BlockSpec(memory_space=pltpu.VMEM)] * count


def smem(count):
    return [pl.BlockSpec(memory_space=pltpu.SMEM)] * count


def chip_body(orbitals, occupations, accumulated):
    _, planes, extent, width = orbitals.shape
    bands, slabs = lax.axis_size("band"), lax.axis_size("slab")
    lines = slabs // 2
    depth = planes // CORES
    band, slab = lax.axis_index("band"), lax.axis_index("slab")
    core, side = band % CORES, slab % 2
    line = slab // 2

    def moved(value, to):
        pairs = []
        for x in range(bands // CORES):
            for c in range(CORES):
                for z in range(lines):
                    for y in range(2):
                        target = to(x, c, z, y)
                        if target is not None:
                            tx, tc, tz, ty = target
                            pairs.append(
                                (
                                    (x * CORES + c) * slabs + z * 2 + y,
                                    (tx * CORES + tc) * slabs + tz * 2 + ty,
                                )
                            )
        return lax.ppermute(value, AXES, pairs)

    over_core = lambda x, c, z, y: (x, c ^ 1, z, y)
    over_x = lambda x, c, z, y: (x ^ 1, c, z, y)
    over_y = lambda x, c, z, y: (x, c, z, y ^ 1)
    over_z = lambda x, c, z, y: (x, c, z ^ 1, y)
    over_middle = lambda x, c, z, y: (x, c, z ^ 3, y) if z in (1, 2) else None
    outward = lambda x, c, z, y: (x, c, z ^ 1, y) if z in (1, 2) else None

    def piece(orbital, half, source=None):
        return lax.dynamic_slice(
            orbitals if source is None else source, (orbital, half * depth, 0, 0), (1, depth, extent, width)
        )[0]

    zero = jnp.int32(0)
    kept_half = piece(zero, core)
    swapped_half = moved(piece(zero, 1 - core), over_core)
    same = core == side
    leads = jnp.stack(
        [jnp.where(same, kept_half, swapped_half), jnp.where(same, swapped_half, kept_half)]
    )

    def shares(bits):
        return moved(occupations[0:1], lambda x, c, z, y: (x ^ (bits // 2), c ^ (bits % 2), z, y))

    all_shares = jnp.concatenate([occupations[0:1]] + [shares(bits) for bits in range(1, bands)])

    def share(x_bit, owner):
        return lax.dynamic_slice(all_shares, (x_bit * 2 + (core ^ owner),), (1,))

    held = [[None, None] for _ in range(lines)]

    def fetch(m, t):
        held[m][t] = moved(
            piece(line ^ m, core ^ side ^ t), lambda x, c, z, y: (x, c ^ y ^ t, z ^ m, c)
        )

    weights = jnp.concatenate([share(0, 1 - side), share(1, side), share(1, 1 - side)])
    orbitals, leads = lax.optimization_barrier((orbitals, leads))
    for m in range(lines):
        for t in range(2):
            fetch(m, t)

    leads_z = moved(leads, over_z)
    far_x = [moved(leads, over_x), moved(leads_z, over_x)]
    leads_z, weights = lax.optimization_barrier((leads_z, weights))
    near = [jnp.stack([leads[row], leads_z[row]]) for row in range(2)]
    inner = [moved(near[row], over_middle) for row in range(2)]
    beside_near = moved(near[0], over_y)
    middle = (line == 1) | (line == 2)
    outer = [moved(inner[row], outward) for row in range(2)]
    far = [jnp.where(middle, inner[row][::-1], outer[row]) for row in range(2)]
    x_near = [jnp.stack([far_x[0][row], far_x[1][row]]) for row in range(2)]
    x_beside_near = moved(beside_near, over_x)
    x_far = [moved(far[row], over_x) for row in range(2)]
    beside_far = moved(far[0], over_y)
    x_mine_beside_near = moved(x_near[1], over_y)
    x_beside_far = moved(beside_far, over_x)
    x_mine_beside_far = moved(x_far[1], over_y)
    visitors = [
        ((near[1], beside_near), (far[1], beside_far)),
        ((x_near[0], x_mine_beside_near), (x_far[0], x_mine_beside_far)),
        ((x_near[1], x_beside_near), (x_far[1], x_beside_far)),
    ]


    natural = jnp.arange(extent, dtype=jnp.int32)
    matrix = hartley_matrix(extent)
    keep = extent // CORES
    order_b = (natural + core * keep) % extent
    steps = jnp.arange(lines, dtype=jnp.int32)
    sides = jnp.arange(2, dtype=jnp.int32)
    offsets = jnp.arange(depth, dtype=jnp.int32)
    spots = (
        (line ^ steps)[:, None, None] * (2 * planes)
        + (side ^ sides)[None, :, None] * planes
        + offsets[None, None, :]
    ).reshape(-1)
    order_x = jnp.concatenate([spots + core * depth, spots + (1 - core) * depth])
    rows_b = hartley_rows(order_b, extent)
    rows_x = hartley_rows(order_x, extent)
    right = right_factor(matrix)
    left_b_forth = left_factor(rows_b)
    left_b_back = left_factor(rows_b.T)
    left_x_forth = left_factor(rows_x.T)
    left_x_back = left_factor(rows_x)
    wave = signed_wave(natural, extent)
    wave_b = signed_wave(order_b[:keep], extent)
    square = wave_b[:, None, None] ** 2 + wave[None, :, None] ** 2 + wave[None, None, :] ** 2
    screen = 4.0 * math.pi / (square + 0.01) / float(extent**3)

    flag = core.reshape(1).astype(jnp.int32)
    group = lines // 2 * 2 * depth
    spectrum_shape = jax.ShapeDtypeStruct((keep, group, width), jnp.float32)
    piece_shape = jax.ShapeDtypeStruct((depth, extent, width), jnp.float32)
    params = pltpu.CompilerParams(vmem_limit_bytes=24 * 1024 * 1024)

    def forward(index, part):
        pieces = [held[m][t] for m in (2 * part, 2 * part + 1) for t in range(2)]
        return pl.pallas_call(
            forward_kernel,
            out_shape=(spectrum_shape, spectrum_shape),
            in_specs=smem(1) + vmem(8),
            out_specs=tuple(vmem(2)),
            compiler_params=params,
            name="forward",
        )(flag, *visitors[index][part], *pieces, right, left_b_forth)

    def across(parts):
        return pl.pallas_call(
            across_kernel,
            out_shape=(spectrum_shape,) * 4,
            in_specs=vmem(7),
            out_specs=tuple(vmem(4)),
            compiler_params=params,
            name="across",
        )(*parts, screen, left_x_forth, left_x_back)

    def inverse(part, spectra):
        operands = []
        for index, pair in enumerate(spectra):
            operands += [*pair, *visitors[index][part]]
        return pl.pallas_call(
            inverse_kernel,
            out_shape=(piece_shape,) * 4,
            in_specs=smem(2) + vmem(len(operands) + 2),
            out_specs=tuple(vmem(4)),
            compiler_params=params,
            name="inverse",
        )(flag, weights, right, left_b_back, *operands)

    spectra = [[], []]
    for index in range(HOPS):
        kept, got = [], []
        for part in range(2):
            own, sent = forward(index, part)
            kept.append(own)
            got.append(moved(sent, over_core))
        out = across(kept + got)
        for part in range(2):
            spectra[part].append((out[part], moved(out[2 + part], over_core)))

    result = accumulated
    for part in (1, 0):
        terms = inverse(part, spectra[part])
        for place in range(2):
            for t in range(2):
                m = 2 * part + place
                back = moved(
                    terms[2 * place + t],
                    lambda x, c, z, y: (x, y, z ^ m, c ^ y ^ t),
                )
                start = (line ^ m, (core ^ side ^ t) * depth, 0, 0)
                old = lax.dynamic_slice(accumulated, start, (1, depth, extent, width))
                result = lax.dynamic_update_slice(result, old - back[None], start)
    return result


def solution(mesh):
    bands, slabs = mesh.shape["band"], mesh.shape["slab"]

    def body(orbitals, occupations, accumulated):
        residents, planes = orbitals.shape[:2]
        one_each = bands == HOPS + 1 and slabs == 2 * residents and residents == 2 * CORES
        if one_each and planes % (8 * CORES) == 0:
            return chip_body(orbitals, occupations, accumulated)
        return slab_body(orbitals, occupations, accumulated)

    in_specs = (P("band", "slab", None, None), P("band"), P("band", "slab", None, None))
    out_specs = P("band", "slab", None, None)
    return jax.shard_map(
        body, mesh=mesh, in_specs=in_specs, out_specs=out_specs, check_vma=False
    )
```

```python
import functools
import math

import jax
import jax.numpy as jnp
from jax import lax
from jax.experimental import pallas as pl
from jax.experimental.pallas import tpu as pltpu
from jax.sharding import PartitionSpec as P


HOPS = 3
CORES = 2
AXES = ("band", "slab")


def shifted(value, axis, steps):
    count = lax.axis_size(axis)
    pairs = [(source, (source + steps) % count) for source in range(count)]
    return lax.ppermute(value, axis, pairs)


def hartley_rows(rows, extent):
    index = jnp.arange(extent, dtype=jnp.int32)
    product = rows[:, None] * index[None, :] % extent
    angle = product.astype(jnp.float32) * (2.0 * math.pi / extent)
    return jnp.cos(angle) + jnp.sin(angle)


def hartley_matrix(extent):
    return hartley_rows(jnp.arange(extent, dtype=jnp.int32), extent)


def signed_wave(index, extent):
    signed = jnp.where(index < extent // 2, index, index - extent)
    return signed.astype(jnp.float32) * (2.0 * math.pi / extent)


def slab_body(orbitals, occupations, accumulated):
    extent = orbitals.shape[2]
    planes = orbitals.shape[1]
    matrix = hartley_matrix(extent)
    full_index = jnp.arange(extent, dtype=jnp.int32)
    local_index = lax.axis_index("slab") * planes + jnp.arange(planes, dtype=jnp.int32)
    wave_full = signed_wave(full_index, extent)
    wave_local = signed_wave(local_index, extent)
    square = (
        wave_full[:, None, None] ** 2
        + wave_local[None, :, None] ** 2
        + wave_full[None, None, :] ** 2
    )
    screening = 4.0 * math.pi / (square + 0.01) / float(extent**3)
    highest = lax.Precision.HIGHEST

    def transform_inner(values):
        spectra = jnp.einsum("pxyz,zc->pxyc", values, matrix, precision=highest)
        return jnp.einsum("pxyc,yb->pxbc", spectra, matrix, precision=highest)

    leading = orbitals[0]
    leading_occ = occupations[0:1]
    carried = (leading, leading_occ)
    visits = []
    for _ in range(HOPS):
        carried = shifted((carried[0], carried[1]), "band", 1)
        visits.append(carried)
    result = accumulated
    for visitor, visitor_occ in visits:
        potentials_spectra = transform_inner(orbitals * visitor[None])
        columns = jnp.einsum(
            "pxbc,xa->pabc",
            lax.all_to_all(potentials_spectra, "slab", split_axis=2, concat_axis=1, tiled=True),
            matrix,
            precision=highest,
        )
        columns = columns * screening[None]
        columns = jnp.einsum("pabc,ax->pxbc", columns, matrix, precision=highest)
        returned = lax.all_to_all(columns, "slab", split_axis=1, concat_axis=2, tiled=True)
        potential = transform_inner(returned)
        result = result - visitor_occ[0] * visitor[None] * potential
    return result


def halves(values):
    head = values.astype(jnp.bfloat16)
    return head, (values - head.astype(jnp.float32)).astype(jnp.bfloat16)


def rounded_halves(matrix):
    head = lax.reduce_precision(matrix, exponent_bits=8, mantissa_bits=7)
    return head.astype(jnp.bfloat16), (matrix - head).astype(jnp.bfloat16)


def right_factor(matrix):
    head, tail = rounded_halves(matrix)
    return jnp.concatenate(
        [
            jnp.concatenate([head, tail], 1),
            jnp.concatenate([head, jnp.zeros_like(tail)], 1),
        ],
        0,
    )


def left_factor(matrix):
    head, tail = rounded_halves(matrix)
    return jnp.concatenate(
        [
            jnp.concatenate([head, head], 1),
            jnp.concatenate([tail, jnp.zeros_like(tail)], 1),
        ],
        0,
    )


def times_right(rows, factor):
    width = rows.shape[1]
    out = jnp.dot(
        jnp.concatenate(halves(rows), 1), factor, preferred_element_type=jnp.float32
    )
    return out[:, :width] + out[:, width:]


def times_left(factor, columns):
    out = jnp.dot(
        factor, jnp.concatenate(halves(columns), 0), preferred_element_type=jnp.float32
    )
    height = out.shape[0] // 2
    return out[:height] + out[height:]


def forward_kernel(flag_ref, own_ref, beside_ref, *refs):
    residents = refs[:4]
    right_ref, left_ref, kept_ref, sent_ref = refs[4:]
    keep = kept_ref.shape[0]
    places, depth, _, width = own_ref.shape
    flip = flag_ref[0] == 1
    for place in range(places):
        first, second = residents[2 * place], residents[2 * place + 1]
        for e in range(2):
            visitor = (own_ref, beside_ref)[e]
            made = []
            for plane in range(0, depth, 2):
                pair = []
                for p in (plane, plane + 1):
                    if e == 0:
                        resident = jnp.where(flip, second[p], first[p])
                    else:
                        resident = jnp.where(flip, first[p], second[p])
                    pair.append(times_right(resident * visitor[place, p], right_ref[...]))
                both = times_left(left_ref[...], jnp.concatenate(pair, 1))
                made.append(both[:, :width])
                made.append(both[:, width:])
            block = jnp.transpose(jnp.stack(made, 0), (1, 0, 2))
            at = (2 * place + e) * depth
            kept_ref[:, at : at + depth, :] = block[:keep]
            sent_ref[:, at : at + depth, :] = block[keep:]


def across_kernel(a_ref, b_ref, c_ref, d_ref, screen_ref, forth_ref, back_ref, *outs):
    parts = (a_ref, b_ref, c_ref, d_ref)
    count, depth, width = a_ref.shape
    for row in range(0, count, 2):
        columns = jnp.concatenate(
            [
                jnp.concatenate([part[row], part[row + 1]], 1)
                for part in parts
            ],
            0,
        )
        spectrum = times_left(forth_ref[...], columns)
        spectrum = spectrum * jnp.concatenate([screen_ref[row], screen_ref[row + 1]], 1)
        lines = times_left(back_ref[...], spectrum)
        for index, out in enumerate(outs):
            out[row] = lines[index * depth : (index + 1) * depth, :width]
            out[row + 1] = lines[index * depth : (index + 1) * depth, width:]


def inverse_kernel(chosen, flag_ref, cross_ref, a_ref, b_ref, c_ref, d_ref, right_ref, left_ref, *refs):
    outs = refs[-2 * len(chosen) :]
    groups = [refs[4 * index : 4 * index + 4] for index in range((len(refs) - len(outs)) // 4)]
    _, depth, extent, width = groups[0][2].shape
    flip = flag_ref[0] == 1
    crossed = cross_ref[0] == 1
    weights = (
        jnp.where(crossed, a_ref[0], b_ref[0]),
        jnp.where(crossed, d_ref[0], c_ref[0]),
        jnp.where(crossed, c_ref[0], d_ref[0]),
    )

    def potentials(own_ref, other_ref, slot):
        at = slice(slot * depth, (slot + 1) * depth)
        rows = jnp.concatenate([own_ref[:, at, :], other_ref[:, at, :]], 0)
        rows = times_right(rows.reshape(extent * depth, width), right_ref[...])
        block = jnp.transpose(rows.reshape(extent, depth, width), (1, 0, 2))
        made = []
        for plane in range(0, depth, 2):
            both = times_left(
                left_ref[...], jnp.concatenate([block[plane], block[plane + 1]], 1)
            )
            made += [both[:, :width], both[:, width:]]
        return made

    for number, place in enumerate(chosen):
        sums = [[None] * depth, [None] * depth]
        for e in range(2):
            for index, (own_ref, other_ref, near_ref, beside_ref) in enumerate(groups):
                made = potentials(own_ref, other_ref, 2 * place + e)
                visitor = (near_ref, beside_ref)[e]
                for p in range(depth):
                    term = weights[index] * visitor[place, p] * made[p]
                    sums[e][p] = term if index == 0 else sums[e][p] + term
        for p in range(depth):
            outs[2 * number][p] = jnp.where(flip, sums[1][p], sums[0][p])
            outs[2 * number + 1][p] = jnp.where(flip, sums[0][p], sums[1][p])


def vmem(count):
    return [pl.BlockSpec(memory_space=pltpu.VMEM)] * count


def smem(count):
    return [pl.BlockSpec(memory_space=pltpu.SMEM)] * count


def chip_body(orbitals, occupations, accumulated):
    _, planes, extent, width = orbitals.shape
    bands, slabs = lax.axis_size("band"), lax.axis_size("slab")
    lines = slabs // 2
    depth = planes // CORES
    band, slab = lax.axis_index("band"), lax.axis_index("slab")
    core, side = band % CORES, slab % 2
    line = slab // 2

    def moved(value, to):
        pairs = []
        for x in range(bands // CORES):
            for c in range(CORES):
                for z in range(lines):
                    for y in range(2):
                        target = to(x, c, z, y)
                        if target is not None:
                            tx, tc, tz, ty = target
                            pairs.append(
                                (
                                    (x * CORES + c) * slabs + z * 2 + y,
                                    (tx * CORES + tc) * slabs + tz * 2 + ty,
                                )
                            )
        return lax.ppermute(value, AXES, pairs)

    over_core = lambda x, c, z, y: (x, c ^ 1, z, y)
    over_x = lambda x, c, z, y: (x ^ 1, c, z, y)
    over_y = lambda x, c, z, y: (x, c, z, y ^ 1)
    over_z = lambda x, c, z, y: (x, c, z ^ 1, y)
    over_middle = lambda x, c, z, y: (x, c, z ^ 3, y) if z in (1, 2) else None
    outward = lambda x, c, z, y: (x, c, z ^ 1, y) if z in (1, 2) else None

    def piece(orbital, half, source=None):
        return lax.dynamic_slice(
            orbitals if source is None else source, (orbital, half * depth, 0, 0), (1, depth, extent, width)
        )[0]

    zero = jnp.int32(0)
    kept_half = piece(zero, core)
    swapped_half = moved(piece(zero, 1 - core), over_core)
    same = core == side
    leads = jnp.stack(
        [jnp.where(same, kept_half, swapped_half), jnp.where(same, swapped_half, kept_half)]
    )

    def shares(bits):
        return moved(occupations[0:1], lambda x, c, z, y: (x ^ (bits // 2), c ^ (bits % 2), z, y))

    all_shares = [occupations[0:1]] + [shares(bits) for bits in range(1, bands)]

    held = [[None, None] for _ in range(lines)]
    middle = (line == 1) | (line == 2)

    def fetch(m, t):
        value = piece(line ^ m, core ^ side ^ t)
        to = lambda x, c, z, y: (x, c ^ y ^ t, z ^ m, c)
        if m < 3:
            held[m][t] = moved(value, to)
            return
        inside = moved(value, lambda x, c, z, y: to(x, c, z, y) if z in (1, 2) else None)
        outside = moved(value, lambda x, c, z, y: to(x, c, z, y) if z in (0, 3) else None)
        held[m][t] = jnp.where(middle, inside, outside)

    orbitals, leads = lax.optimization_barrier((orbitals, leads))
    for m in range(lines):
        for t in range(2):
            fetch(m, t)

    leads_z = moved(leads, over_z)
    far_x = [moved(leads, over_x), moved(leads_z, over_x)]
    near = [jnp.stack([leads[row], leads_z[row]]) for row in range(2)]
    inner = [moved(near[row], over_middle) for row in range(2)]
    beside_near = moved(near[0], over_y)
    outer = [moved(inner[row], outward) for row in range(2)]
    far = [jnp.where(middle, inner[row][::-1], outer[row]) for row in range(2)]
    x_near = [jnp.stack([far_x[0][row], far_x[1][row]]) for row in range(2)]
    x_beside_near = moved(beside_near, over_x)
    x_far = [moved(far[row], over_x) for row in range(2)]
    beside_far = moved(far[0], over_y)
    x_mine_beside_near = moved(x_near[1], over_y)
    x_beside_far = moved(beside_far, over_x)
    x_mine_beside_far = moved(x_far[1], over_y)
    visitors = [
        ((near[1], beside_near), (far[1], beside_far)),
        ((x_near[0], x_mine_beside_near), (x_far[0], x_mine_beside_far)),
        ((x_near[1], x_beside_near), (x_far[1], x_beside_far)),
    ]


    natural = jnp.arange(extent, dtype=jnp.int32)
    matrix = hartley_matrix(extent)
    keep = extent // CORES
    order_b = (natural + core * keep) % extent
    steps = jnp.arange(lines, dtype=jnp.int32)
    sides = jnp.arange(2, dtype=jnp.int32)
    offsets = jnp.arange(depth, dtype=jnp.int32)
    spots = (
        (line ^ steps)[:, None, None] * (2 * planes)
        + (side ^ sides)[None, :, None] * planes
        + offsets[None, None, :]
    ).reshape(-1)
    order_x = jnp.concatenate([spots + core * depth, spots + (1 - core) * depth])
    rows_b = hartley_rows(order_b, extent)
    rows_x = hartley_rows(order_x, extent)
    right = right_factor(matrix)
    left_b_forth = left_factor(rows_b)
    left_b_back = left_factor(rows_b.T)
    left_x_forth = left_factor(rows_x.T)
    left_x_back = left_factor(rows_x)
    wave = signed_wave(natural, extent)
    wave_b = signed_wave(order_b[:keep], extent)
    square = wave_b[:, None, None] ** 2 + wave[None, :, None] ** 2 + wave[None, None, :] ** 2
    screen = 4.0 * math.pi / (square + 0.01) / float(extent**3)

    flag = core.reshape(1).astype(jnp.int32)
    cross = (core ^ side).reshape(1).astype(jnp.int32)
    group = lines // 2 * 2 * depth
    spectrum_shape = jax.ShapeDtypeStruct((keep, group, width), jnp.float32)
    piece_shape = jax.ShapeDtypeStruct((depth, extent, width), jnp.float32)
    params = pltpu.CompilerParams(vmem_limit_bytes=24 * 1024 * 1024)

    def forward(index, part):
        pieces = [held[m][t] for m in (2 * part, 2 * part + 1) for t in range(2)]
        return pl.pallas_call(
            forward_kernel,
            out_shape=(spectrum_shape, spectrum_shape),
            in_specs=smem(1) + vmem(8),
            out_specs=tuple(vmem(2)),
            compiler_params=params,
            name="forward",
        )(flag, *visitors[index][part], *pieces, right, left_b_forth)

    def across(parts):
        return pl.pallas_call(
            across_kernel,
            out_shape=(spectrum_shape,) * 4,
            in_specs=vmem(7),
            out_specs=tuple(vmem(4)),
            compiler_params=params,
            name="across",
        )(*parts, screen, left_x_forth, left_x_back)

    def inverse(part, chosen, spectra):
        operands = []
        for index, pair in enumerate(spectra):
            operands += [*pair, *visitors[index][part]]
        return pl.pallas_call(
            functools.partial(inverse_kernel, chosen),
            out_shape=(piece_shape,) * (2 * len(chosen)),
            in_specs=smem(2 + bands) + vmem(len(operands) + 2),
            out_specs=tuple(vmem(2 * len(chosen))),
            compiler_params=params,
            name="inverse",
        )(flag, cross, *all_shares, right, left_b_back, *operands)

    spectra = [[], []]
    for index in range(HOPS):
        kept, got = [], []
        for part in range(2):
            own, sent = forward(index, part)
            kept.append(own)
            got.append(moved(sent, over_core))
        out = across(kept + got)
        for part in range(2):
            spectra[part].append((out[part], moved(out[2 + part], over_core)))

    result = accumulated
    for part, chosen in ((1, (0,)), (1, (1,)), (0, (0, 1))):
        terms = inverse(part, chosen, spectra[part])
        for number, place in enumerate(chosen):
            for t in range(2):
                m = 2 * part + place
                back = moved(terms[2 * number + t], lambda x, c, z, y: (x, y, z ^ m, c ^ y ^ t))
                start = (line ^ m, (core ^ side ^ t) * depth, 0, 0)
                old = lax.dynamic_slice(accumulated, start, (1, depth, extent, width))
                result = lax.dynamic_update_slice(result, old - back[None], start)
    return result


def solution(mesh):
    bands, slabs = mesh.shape["band"], mesh.shape["slab"]

    def body(orbitals, occupations, accumulated):
        residents, planes = orbitals.shape[:2]
        one_each = bands == HOPS + 1 and slabs == 2 * residents and residents == 2 * CORES
        if one_each and planes % (8 * CORES) == 0:
            return chip_body(orbitals, occupations, accumulated)
        return slab_body(orbitals, occupations, accumulated)

    in_specs = (P("band", "slab", None, None), P("band"), P("band", "slab", None, None))
    out_specs = P("band", "slab", None, None)
    return jax.shard_map(
        body, mesh=mesh, in_specs=in_specs, out_specs=out_specs, check_vma=False
    )
```
